32 devices in a mesh: seek: 4 (over z), emp: 8 (over y, x, core).
Axes of the slice: x: 2, y: 2, z: 4, core: 2. Of those that a mesh axis runs over, the one named last changes fastest.
Arguments:
- seek_region: int32 [64], replicated, may hold values from 0 to 7, as said below
- emp_region: int32 [64], replicated, may hold values from 0 to 7
- seeker_emb: bfloat16 [32768, 256], P('seek'), may hold values from -52 to 52
- employer_emb: bfloat16 [32768, 256], P('emp'), may hold values from -6 to 6
- bilinear: bfloat16 [256, 256], replicated, may hold values from -0.375 to 0.375
- logged_emp: int32 [32768], P('seek'), may hold values from 0 to 32767, as said below
- logged_seeker: int32 [32768], P('emp'), may hold values from 0 to 32767, as said below
- seek_weight: float32 [32768], P('seek'), may hold values from 0.2 to 5
- emp_weight: float32 [32768], P('emp'), may hold values from 0.2 to 5
Outputs:
- seeker_grad: float32 [32768, 256], P(('seek', 'emp'))
- employer_grad: float32 [32768, 256], P(('emp', 'seek'))
- bilinear_grad: float32 [256, 256], replicated
The draws below stay inside these ranges and needn't reach their ends.
Inputs may be any that keep to these rules, and one draw needn't show every extreme that they name: `seek_region`: every region holds at least one seeker block and one employer block. `logged_emp`: each seeker's logged employer lies in a block of the seeker's region. `logged_seeker`: each employer's logged seeker lies in a block of the employer's region.
All inputs are finite; a program needn't handle non-finite values.
Results may differ from the reference program's by a relative error of at most 0.012.
The reference program's roundings to bfloat16 on the way (of `proj`, `dscore` and `pulled`) count: a program that leaves them out, or rounds other values in their place, can miss the bound.
Values sent between devices are 32-bit elements; how exact they have to be, the bound alone decides.
A program may use at most 128 MiB of HBM per device.

```python
import math
import jax
import jax.numpy as jnp
from jax import lax

E = 256
BLK = 512
REGIONS = 8
SEEK_BLOCKS = 64
EMP_BLOCKS = 64
SEEKERS = 32768
EMPLOYERS = 32768


def region_list(key_low, key_high, key_order, count):
    base = jnp.minimum(jax.random.randint(key_low, (count,), 0, REGIONS), jax.random.randint(key_high, (count,), 0, REGIONS))
    order = jax.random.permutation(key_order, count)
    return base.at[order[:REGIONS]].set(jnp.arange(REGIONS, dtype=jnp.int32)).astype(jnp.int32)


def region_tables(key):
    seek = region_list(jax.random.fold_in(key, 11), jax.random.fold_in(key, 12), jax.random.fold_in(key, 13), SEEK_BLOCKS)
    emp = region_list(jax.random.fold_in(key, 21), jax.random.fold_in(key, 22), jax.random.fold_in(key, 23), EMP_BLOCKS)
    return (seek, emp)


def draw_seek_region(key, part):
    return region_tables(key)[0]


def draw_emp_region(key, part):
    return region_tables(key)[1]


def pick_match(key, own_regions, other_regions, own_count, other_blocks):
    region_rows = jnp.repeat(own_regions, BLK)
    marks = jax.random.randint(jax.random.fold_in(key, 1), (own_count, other_blocks), 0, 2 ** 20) * other_blocks
    marks = marks + jnp.arange(other_blocks, dtype=jnp.int32)[None, :]
    marks = jnp.where(other_regions[None, :] == region_rows[:, None], marks, -1)
    chosen = jnp.argmax(marks, axis=1).astype(jnp.int32)
    offset = jax.random.randint(jax.random.fold_in(key, 2), (own_count,), 0, BLK)
    return (chosen * BLK + offset).astype(jnp.int32)


def draw_logged_emp(key, part):
    seek, emp = region_tables(key)
    return pick_match(jax.random.fold_in(key, 31), seek, emp, SEEKERS, EMP_BLOCKS)


def draw_logged_seeker(key, part):
    seek, emp = region_tables(key)
    return pick_match(jax.random.fold_in(key, 41), emp, seek, EMPLOYERS, SEEK_BLOCKS)


def draw_seeker_emb(key, part):
    values = jnp.clip(jax.random.normal(jax.random.fold_in(key, 53), (SEEKERS, E), jnp.float32), -6.0, 6.0)
    return values.astype(jnp.bfloat16)


def block_scale(key, shape, cuts, least, largest):
    def one(axis_at, parts):
        heights = jax.random.uniform(jax.random.fold_in(jax.random.fold_in(key, 6), axis_at), (parts,), jnp.float32, least / len(cuts), largest / len(cuts))
        return jnp.repeat(jnp.exp(heights), shape[axis_at] // parts).reshape((-1,) + (1,) * (len(shape) - axis_at - 1))

    level = one(*cuts[0])
    for cut in cuts[1:]:
        level = level * one(*cut)
    return level


def centred(own_key, dims, deviation, bound, pieces=(), held_as=jnp.bfloat16):
    values = deviation * jax.random.normal(own_key, dims, jnp.float32)
    if pieces:
        values = values * block_scale(own_key, dims, pieces, -0.22, 0.18)
    return jnp.clip(values, -bound, bound).astype(held_as)


def setup_inputs(seed: int = 0) -> dict:
    keys = jax.random.split(jax.random.key(seed), 10)
    return {
        "seek_region": draw_seek_region(jax.random.fold_in(keys[9], 71), 0),
        "emp_region": draw_emp_region(jax.random.fold_in(keys[9], 71), 0),
        "seeker_emb": draw_seeker_emb(jax.random.fold_in(keys[9], 71), 0),
        "employer_emb": centred(keys[3], (EMPLOYERS, E), 1.0, 6.0, ((0, 8),)),
        "bilinear": centred(keys[4], (E, E), E ** -0.5, 0.375),
        "logged_emp": draw_logged_emp(jax.random.fold_in(keys[9], 71), 0),
        "logged_seeker": draw_logged_seeker(jax.random.fold_in(keys[9], 71), 0),
        "seek_weight": jnp.clip(jnp.exp(math.log(5.0) - 3.218876 * jax.random.uniform(keys[7], (SEEKERS,), jnp.float32) ** block_scale(keys[7], (SEEKERS,), ((0, 4),), -0.2, 0.2)), 0.2, 5.0),
        "emp_weight": jnp.clip(jnp.exp(math.log(5.0) - 3.218876 * jax.random.uniform(keys[8], (EMPLOYERS,), jnp.float32) ** block_scale(keys[8], (EMPLOYERS,), ((0, 8),), -0.2, 0.2)), 0.2, 5.0),
    }


big_value = 1.0e30


def reference(seek_region, emp_region, seeker_emb, employer_emb, bilinear, logged_emp, logged_seeker, seek_weight, emp_weight):
    seekers = seeker_emb.shape[0]
    employers = employer_emb.shape[0]
    nblocks = seekers // BLK
    scale = E ** -0.5
    proj = jnp.dot(seeker_emb, bilinear, preferred_element_type=jnp.float32).astype(jnp.bfloat16)
    emp_regions = jnp.repeat(emp_region, BLK)
    block_ids = jnp.arange(nblocks, dtype=jnp.int32)
    proj_blocks = proj.reshape(nblocks, BLK, E)
    columns = jnp.arange(employers, dtype=jnp.int32)

    def masked_scores(index, rows):
        raw = lax.dot_general(rows, employer_emb, (((1,), (1,)), ((), ())), preferred_element_type=jnp.float32) * scale
        keep = (seek_region[index] == emp_regions)[None, :]
        return jnp.where(keep, raw, -big_value), keep

    def first_pass(carry, xs):
        index, rows = xs
        masked, keep = masked_scores(index, rows)
        top = jnp.max(masked, axis=1)
        total = jnp.sum(jnp.where(keep, jnp.exp(masked - top[:, None]), 0.0), axis=1)
        ctop = jnp.max(masked, axis=0)
        ctotal = jnp.sum(jnp.where(keep, jnp.exp(masked - ctop[None, :]), 0.0), axis=0)
        old_top, old_total = carry
        new_top = jnp.maximum(old_top, ctop)
        new_total = old_total * jnp.exp(old_top - new_top) + ctotal * jnp.exp(ctop - new_top)
        return (new_top, new_total), (top, total)

    init = (jnp.full((employers,), -big_value, jnp.float32), jnp.zeros((employers,), jnp.float32))
    (col_top, col_total), (row_top, row_total) = lax.scan(first_pass, init, (block_ids, proj_blocks))

    def second_pass(carry, xs):
        index, rows, top, total, logged_rows, weight_rows = xs
        masked, keep = masked_scores(index, rows)
        row_hit = (logged_rows[:, None] == columns[None, :]).astype(jnp.float32)
        seek_ids = index * BLK + jnp.arange(BLK, dtype=jnp.int32)
        col_hit = (logged_seeker[None, :] == seek_ids[:, None]).astype(jnp.float32)
        policy = jnp.exp(masked - top[:, None]) / total[:, None]
        other = jnp.exp(masked - col_top[None, :]) / col_total[None, :]
        grad = weight_rows[:, None] * (policy - row_hit) + emp_weight[None, :] * (other - col_hit)
        dscore = (jnp.where(keep, grad, 0.0) * scale).astype(jnp.bfloat16)
        pulled = jnp.dot(dscore, employer_emb, preferred_element_type=jnp.float32)
        carry = carry + lax.dot_general(dscore, rows, (((0,), (0,)), ((), ())), preferred_element_type=jnp.float32)
        return carry, pulled

    xs = (block_ids, proj_blocks, row_top, row_total, logged_emp.reshape(nblocks, BLK), seek_weight.reshape(nblocks, BLK))
    employer_grad, pulled = lax.scan(second_pass, jnp.zeros((employers, E), jnp.float32), xs)
    pulled = pulled.reshape(seekers, E).astype(jnp.bfloat16)
    seeker_grad = lax.dot_general(pulled, bilinear, (((1,), (1,)), ((), ())), preferred_element_type=jnp.float32)
    bilinear_grad = lax.dot_general(seeker_emb, pulled, (((0,), (0,)), ((), ())), preferred_element_type=jnp.float32)
    return seeker_grad, employer_grad, bilinear_grad
```

```python
import functools

import jax
import jax.numpy as jnp
from jax import lax
from jax.experimental import pallas as pl
from jax.experimental.pallas import tpu as pltpu
from jax.sharding import PartitionSpec as P

E = 256
BLK = 512
LANES = 128
ROWS = 64
GROUPS = BLK // LANES
LOW = -1.0e30
TO_LOG2 = 1.4426950408889634 * E ** (-0.5)
VMEM_LIMIT = 56 * 1024 * 1024


def nt_dot(a, b):
    return lax.dot_general(a, b, (((1,), (1,)), ((), ())), preferred_element_type=jnp.float32)


def tn_dot(a, b):
    return lax.dot_general(a, b, (((0,), (0,)), ((), ())), preferred_element_type=jnp.float32)


def block_ds(index, size):
    return pl.ds(pl.multiple_of(index * size, size), size)


def stats_kernel(
    nblocks, eblocks, flags, seeker, employer, bilinear,
    proj, row_stats, col_stats,
    score, row_max, row_sum, col_max, col_sum,
):
    col_max[...] = jnp.full_like(col_max, LOW)
    col_sum[...] = jnp.zeros_like(col_sum)

    def per_row(i, carry):
        rows_at = block_ds(i, BLK)
        proj[rows_at, :] = jnp.dot(
            seeker[rows_at, :], bilinear[...], preferred_element_type=jnp.float32
        ).astype(jnp.bfloat16)
        row_max[...] = jnp.full_like(row_max, LOW)
        row_sum[...] = jnp.zeros_like(row_sum)

        def per_col(j, carry):
            @pl.when(flags[i * eblocks + j] != 0)
            def _():
                cols = employer[block_ds(j, BLK), :]
                half = BLK // 2
                for h in range(2):
                    left = proj[pl.ds(pl.multiple_of(i * BLK + h * half, half), half), :]
                    score[h * half : (h + 1) * half, :] = nt_dot(left, cols)
                cm = col_max[j]
                cs = col_sum[j]
                for c in range(BLK // ROWS):
                    part = slice(c * ROWS, (c + 1) * ROWS)
                    s = score[part, :] * TO_LOG2
                    tall = s.reshape(ROWS // 8, 8, BLK)
                    cm_new = jnp.maximum(cm, jnp.max(tall, axis=0))
                    cs = cs * jnp.exp2(cm - cm_new) + jnp.sum(
                        jnp.exp2(tall - cm_new[None]), axis=0
                    )
                    cm = cm_new
                    old = row_max[part, :]
                    pieces = [s[:, g * LANES : (g + 1) * LANES] for g in range(GROUPS)]
                    new = functools.reduce(jnp.maximum, pieces, old)
                    total = row_sum[part, :] * jnp.exp2(old - new)
                    for piece in pieces:
                        total = total + jnp.exp2(piece - new)
                    row_max[part, :] = new
                    row_sum[part, :] = total
                col_max[j] = cm
                col_sum[j] = cs

            return carry

        lax.fori_loop(0, eblocks, per_col, 0)
        lane_max = row_max[...]
        top = jnp.max(lane_max, axis=1, keepdims=True)
        total = jnp.sum(row_sum[...] * jnp.exp2(lane_max - top), axis=1, keepdims=True)
        row_stats[0, pl.ds(i, 1), :] = jnp.broadcast_to(top, (BLK, LANES)).T[0:1]
        row_stats[1, pl.ds(i, 1), :] = jnp.broadcast_to(total, (BLK, LANES)).T[0:1]
        return carry

    lax.fori_loop(0, nblocks, per_row, 0)
    for j in range(eblocks):
        cm = col_max[j]
        top = jnp.max(cm, axis=0, keepdims=True)
        total = jnp.sum(col_sum[j] * jnp.exp2(cm - top), axis=0, keepdims=True)
        col_stats[0, j : j + 1, :] = top
        col_stats[1, j : j + 1, :] = total


def entry_barrier(n_seek, n_emp, me_s, me_e):
    barrier = pltpu.get_barrier_semaphore()
    for k in range(1, n_emp):
        pl.semaphore_signal(
            barrier, inc=1, device_id={"emp": lax.rem(me_e + k, n_emp)},
            device_id_type=pl.DeviceIdType.MESH,
        )
    for k in range(1, n_seek):
        pl.semaphore_signal(
            barrier, inc=1, device_id={"seek": lax.rem(me_s + k, n_seek)},
            device_id_type=pl.DeviceIdType.MESH,
        )
    pl.semaphore_wait(barrier, n_emp + n_seek - 2)


def send(src, dst, send_sem, recv_sem, axis, peer):
    return pltpu.make_async_remote_copy(
        src_ref=src, dst_ref=dst, send_sem=send_sem, recv_sem=recv_sem,
        device_id={axis: peer}, device_id_type=pl.DeviceIdType.MESH,
    )


def exchange_kernel(
    n_seek, n_emp, row_stats, col_stats, row_weight, col_weight,
    row_top, row_coef, col_top, col_coef,
    row_buf, col_buf, row_send, row_recv, col_send, col_recv,
):
    me_s = lax.axis_index("seek")
    me_e = lax.axis_index("emp")
    entry_barrier(n_seek, n_emp, me_s, me_e)
    copies = []
    for k in range(1, n_emp):
        copies.append(send(
            row_stats, row_buf.at[k], row_send.at[k], row_recv.at[k],
            "emp", lax.rem(me_e + k, n_emp),
        ))
    for k in range(1, n_seek):
        copies.append(send(
            col_stats, col_buf.at[k], col_send.at[k], col_recv.at[k],
            "seek", lax.rem(me_s + k, n_seek),
        ))
    for copy in copies:
        copy.start()
    for copy in copies:
        copy.wait()
    for own, buf, n, weight, top_out, coef_out in (
        (row_stats, row_buf, n_emp, row_weight, row_top, row_coef),
        (col_stats, col_buf, n_seek, col_weight, col_top, col_coef),
    ):
        top = own[0]
        for k in range(1, n):
            top = jnp.maximum(top, buf[k, 0])
        total = own[1] * jnp.exp2(own[0] - top)
        for k in range(1, n):
            total = total + buf[k, 1] * jnp.exp2(buf[k, 0] - top)
        top_out[...] = top
        coef_out[...] = weight[...] / total


def grad_kernel(
    nblocks, eblocks, flags, proj, employer,
    row_top, row_coef, row_weight, row_log, col_top, col_coef, col_weight, col_log,
    pulled, back,
    score, dscore, rt, rc, rw, rl,
):
    back[...] = jnp.zeros_like(back)
    row_ids = lax.broadcasted_iota(jnp.int32, (ROWS, LANES), 0).astype(jnp.float32)
    lane_ids = lax.broadcasted_iota(jnp.int32, (8, LANES), 1).astype(jnp.float32)[0:1]

    def per_row(i, carry):
        rows_at = block_ds(i, BLK)
        pulled[rows_at, :] = jnp.zeros((BLK, E), jnp.float32)
        for source, wide in ((row_top, rt), (row_coef, rc), (row_weight, rw), (row_log, rl)):
            wide[...] = jnp.broadcast_to(source[pl.ds(i, 1), :], (LANES, BLK)).T

        def per_col(j, carry):
            @pl.when(flags[i * eblocks + j] != 0)
            def _():
                cols_at = block_ds(j, BLK)
                cols = employer[cols_at, :]
                half = BLK // 2
                for h in range(2):
                    left = proj[pl.ds(pl.multiple_of(i * BLK + h * half, half), half), :]
                    score[h * half : (h + 1) * half, :] = nt_dot(left, cols)
                ct = col_top[pl.ds(j, 1), :]
                cc = col_coef[pl.ds(j, 1), :]
                cw = col_weight[pl.ds(j, 1), :]
                cl = col_log[pl.ds(j, 1), :] - (i * BLK).astype(jnp.float32)
                here = lane_ids + (j * BLK).astype(jnp.float32)
                for c in range(BLK // ROWS):
                    part = slice(c * ROWS, (c + 1) * ROWS)
                    rtc, rcc, rwc, rlc = (ref[part, :] for ref in (rt, rc, rw, rl))
                    clc = cl - float(c * ROWS)
                    for g in range(GROUPS):
                        lanes = slice(g * LANES, (g + 1) * LANES)
                        t = score[part, lanes] * TO_LOG2
                        grad = jnp.exp2(t - rtc) * rcc + jnp.exp2(t - ct[:, lanes]) * cc[:, lanes]
                        grad = jnp.where(rlc == here + float(g * LANES), grad - rwc, grad)
                        grad = jnp.where(clc[:, lanes] == row_ids, grad - cw[:, lanes], grad)
                        dscore[part, lanes] = grad.astype(jnp.bfloat16)
                d = dscore[...]
                pulled[rows_at, :] += jnp.dot(d, cols, preferred_element_type=jnp.float32)
                back[cols_at, :] += tn_dot(d, proj[rows_at, :])

            return carry

        lax.fori_loop(0, eblocks, per_col, 0)
        return carry

    lax.fori_loop(0, nblocks, per_row, 0)


def reduce_kernel(
    n_seek, n_emp, pulled, back, own_rows, bilinear,
    seeker_grad, employer_grad, bilinear_grad,
    pair_buf, emp_buf, right_buf, left_buf, bil, bil_emp, bil_seek, bil_all,
    pair_send, pair_recv, emp_send, emp_recv, right_send, right_recv, left_send, left_recv,
    b1_send, b1_recv, b2_send, b2_recv, b3_send, b3_recv,
):
    me_s = lax.axis_index("seek")
    me_e = lax.axis_index("emp")
    share = pulled.shape[0] // n_emp
    eshare = back.shape[0] // n_seek
    half = n_emp // 2
    mine = me_e // 2
    parity = lax.rem(me_e, 2)
    partner = me_e + 1 - 2 * parity
    mirror = n_seek - 1 - me_s
    entry_barrier(n_seek, n_emp, me_s, me_e)

    def right_copy(k, src):
        return send(
            src, right_buf.at[k], right_send.at[k], right_recv.at[k],
            "seek", lax.rem(me_s + 1, n_seek),
        )

    def left_copy(k, src):
        return send(
            src, left_buf.at[k], left_send.at[k], left_recv.at[k],
            "seek", lax.rem(me_s + n_seek - 1, n_seek),
        )

    def line_step(k):
        for pos, make, buf, target in (
            (me_s, right_copy, right_buf, n_seek - 1 - k + me_s),
            (mirror, left_copy, left_buf, k - mirror),
        ):
            @pl.when(pos == 0)
            def _(make=make, target=target):
                make(k, back.at[block_ds(target, eshare), :]).start()

            if k > 0:
                @pl.when(jnp.logical_and(pos > 0, pos <= k))
                def _(make=make, buf=buf, target=target):
                    make(k - 1, buf.at[k - 1]).wait_recv()
                    buf[k - 1] += back[block_ds(target, eshare), :]
                    make(k, buf.at[k - 1]).start()

    line_step(0)
    pairs = []
    order = list(range(half - 1, -1, -1))
    for k in range(half):
        target = 2 * lax.rem(mine + k, half) + 1 - parity
        pairs.append(send(
            pulled.at[block_ds(target, share), :], pair_buf.at[k],
            pair_send.at[k], pair_recv.at[k], "emp", partner,
        ))
    for k in order:
        pairs[k].start()
    seconds = {}
    for k in order:
        pairs[k].wait_recv()
        target = 2 * lax.rem(mine + k, half) + parity
        pair_buf[k] += pulled[block_ds(target, share), :]
        if k > 0:
            seconds[k] = send(
                pair_buf.at[k], emp_buf.at[k], emp_send.at[k], emp_recv.at[k], "emp", target
            )
            seconds[k].start()
    for k in range(1, n_seek - 1):
        line_step(k)
    for k in seconds:
        seconds[k].wait_recv()
        pair_buf[0] += emp_buf[k]

    share_rows = pair_buf[0].astype(jnp.bfloat16)
    bil[...] = tn_dot(own_rows[...], share_rows)
    slab = E // n_emp
    b1 = []
    for k in range(1, n_emp):
        peer = lax.rem(me_e + k, n_emp)
        b1.append(send(
            bil.at[block_ds(peer, slab), :], bil_emp.at[k], b1_send.at[k], b1_recv.at[k],
            "emp", peer,
        ))
    for copy in b1:
        copy.start()
    seeker_grad[...] = nt_dot(share_rows, bilinear[...])
    own_slab = block_ds(me_e, slab)
    for copy in b1:
        copy.wait_recv()
    part = bil[own_slab, :]
    for k in range(1, n_emp):
        part = part + bil_emp[k]
    bil_seek[me_s] = part
    b2 = []
    for k in range(1, n_seek):
        b2.append(send(
            bil_seek.at[me_s], bil_seek.at[me_s], b2_send.at[k], b2_recv.at[k],
            "seek", lax.rem(me_s + k, n_seek),
        ))
    for copy in b2:
        copy.start()
    for k in range(1, n_seek):
        slot = bil_seek.at[lax.rem(me_s + n_seek - k, n_seek)]
        send(
            slot, slot, b2_send.at[k], b2_recv.at[k], "seek", lax.rem(me_s + k, n_seek)
        ).wait_recv()
    part = bil_seek[0]
    for k in range(1, n_seek):
        part = part + bil_seek[k]
    bil_all[own_slab, :] = part
    b3 = []
    for k in range(1, n_emp):
        b3.append(send(
            bil_all.at[own_slab, :], bil_all.at[own_slab, :], b3_send.at[k], b3_recv.at[k],
            "emp", lax.rem(me_e + k, n_emp),
        ))
    for copy in b3:
        copy.start()
    for k in range(1, n_emp):
        slot = bil_all.at[block_ds(lax.rem(me_e + n_emp - k, n_emp), slab), :]
        send(
            slot, slot, b3_send.at[k], b3_recv.at[k], "emp", lax.rem(me_e + k, n_emp)
        ).wait_recv()
    bilinear_grad[...] = bil_all[...]

    employer_grad[...] = back[block_ds(me_s, eshare), :]
    last = n_seek - 2
    for pos, make, buf in ((me_s, right_copy, right_buf), (mirror, left_copy, left_buf)):
        @pl.when(pos > 0)
        def _(make=make, buf=buf):
            make(last, buf.at[last]).wait_recv()
            employer_grad[...] += buf[last]

    for copy in pairs + list(seconds.values()) + b1 + b2 + b3:
        copy.wait_send()
    for k in range(n_seek - 1):
        for pos, make, buf in ((me_s, right_copy, right_buf), (mirror, left_copy, left_buf)):
            @pl.when(pos <= k)
            def _(k=k, make=make, buf=buf):
                make(k, buf.at[k]).wait_send()


def vmem():
    return pl.BlockSpec(memory_space=pltpu.VMEM)


def smem():
    return pl.BlockSpec(memory_space=pltpu.SMEM)


def f32(*shape):
    return jax.ShapeDtypeStruct(shape, jnp.float32)


def body(
    n_seek, n_emp, seek_region, emp_region, seeker_emb, employer_emb, bilinear,
    logged_emp, logged_seeker, seek_weight, emp_weight,
):
    seek_pos = lax.axis_index("seek")
    emp_pos = lax.axis_index("emp")
    seekers = seeker_emb.shape[0]
    employers = employer_emb.shape[0]
    nblocks = seekers // BLK
    eblocks = employers // BLK
    own_seek = lax.dynamic_slice_in_dim(seek_region, seek_pos * nblocks, nblocks)
    own_emp = lax.dynamic_slice_in_dim(emp_region, emp_pos * eblocks, eblocks)
    flags = (own_seek[:, None] == own_emp[None, :]).astype(jnp.int32).reshape(-1)
    row_log = (logged_emp - emp_pos * employers).astype(jnp.float32).reshape(nblocks, BLK)
    col_log = (logged_seeker - seek_pos * seekers).astype(jnp.float32).reshape(eblocks, BLK)
    scale = E ** (-0.5)
    row_weight = (seek_weight * scale).reshape(nblocks, BLK)
    col_weight = (emp_weight * scale).reshape(eblocks, BLK)

    proj, row_stats, col_stats = pl.pallas_call(
        functools.partial(stats_kernel, nblocks, eblocks),
        out_shape=(
            jax.ShapeDtypeStruct((seekers, E), jnp.bfloat16),
            f32(2, nblocks, BLK),
            f32(2, eblocks, BLK),
        ),
        in_specs=[smem()] + [vmem()] * 3,
        out_specs=(vmem(),) * 3,
        scratch_shapes=[
            pltpu.VMEM((BLK, BLK), jnp.float32),
            pltpu.VMEM((BLK, LANES), jnp.float32),
            pltpu.VMEM((BLK, LANES), jnp.float32),
            pltpu.VMEM((eblocks, 8, BLK), jnp.float32),
            pltpu.VMEM((eblocks, 8, BLK), jnp.float32),
        ],
        compiler_params=pltpu.CompilerParams(vmem_limit_bytes=VMEM_LIMIT),
        name="stats",
    )(flags, seeker_emb, employer_emb, bilinear)

    row_top, row_coef, col_top, col_coef = pl.pallas_call(
        functools.partial(exchange_kernel, n_seek, n_emp),
        out_shape=(f32(nblocks, BLK), f32(nblocks, BLK), f32(eblocks, BLK), f32(eblocks, BLK)),
        in_specs=[vmem()] * 4,
        out_specs=(vmem(),) * 4,
        scratch_shapes=[
            pltpu.VMEM((n_emp, 2, nblocks, BLK), jnp.float32),
            pltpu.VMEM((n_seek, 2, eblocks, BLK), jnp.float32),
            pltpu.SemaphoreType.DMA((n_emp,)),
            pltpu.SemaphoreType.DMA((n_emp,)),
            pltpu.SemaphoreType.DMA((n_seek,)),
            pltpu.SemaphoreType.DMA((n_seek,)),
        ],
        compiler_params=pltpu.CompilerParams(collective_id=0, has_side_effects=True),
        name="exchange",
    )(row_stats, col_stats, row_weight, col_weight)

    pulled, back = pl.pallas_call(
        functools.partial(grad_kernel, nblocks, eblocks),
        out_shape=(f32(seekers, E), f32(employers, E)),
        in_specs=[smem()] + [vmem()] * 10,
        out_specs=(vmem(),) * 2,
        scratch_shapes=[
            pltpu.VMEM((BLK, BLK), jnp.float32),
            pltpu.VMEM((BLK, BLK), jnp.bfloat16),
        ]
        + [pltpu.VMEM((BLK, LANES), jnp.float32)] * 4,
        compiler_params=pltpu.CompilerParams(vmem_limit_bytes=VMEM_LIMIT),
        name="grads",
    )(
        flags, proj, employer_emb,
        row_top, row_coef, row_weight, row_log, col_top, col_coef, col_weight, col_log,
    )

    share = seekers // n_emp
    eshare = employers // n_seek
    own_rows = lax.dynamic_slice_in_dim(seeker_emb, emp_pos * share, share, 0)
    slab = E // n_emp
    dma = pltpu.SemaphoreType.DMA
    return pl.pallas_call(
        functools.partial(reduce_kernel, n_seek, n_emp),
        out_shape=(f32(share, E), f32(eshare, E), f32(E, E)),
        in_specs=[vmem()] * 4,
        out_specs=(vmem(),) * 3,
        scratch_shapes=[
            pltpu.VMEM((n_emp // 2, share, E), jnp.float32),
            pltpu.VMEM((n_emp // 2, share, E), jnp.float32),
            pltpu.VMEM((n_seek - 1, eshare, E), jnp.float32),
            pltpu.VMEM((n_seek - 1, eshare, E), jnp.float32),
            pltpu.VMEM((E, E), jnp.float32),
            pltpu.VMEM((n_emp, slab, E), jnp.float32),
            pltpu.VMEM((n_seek, slab, E), jnp.float32),
            pltpu.VMEM((E, E), jnp.float32),
            dma((n_emp // 2,)), dma((n_emp // 2,)),
            dma((n_emp // 2,)), dma((n_emp // 2,)),
            dma((n_seek - 1,)), dma((n_seek - 1,)),
            dma((n_seek - 1,)), dma((n_seek - 1,)),
            dma((n_emp,)), dma((n_emp,)),
            dma((n_seek,)), dma((n_seek,)),
            dma((n_emp,)), dma((n_emp,)),
        ],
        compiler_params=pltpu.CompilerParams(
            collective_id=1, has_side_effects=True, vmem_limit_bytes=VMEM_LIMIT
        ),
        name="reduce",
    )(pulled, back, own_rows, bilinear)


def solution(mesh):
    return jax.shard_map(
        functools.partial(body, mesh.shape["seek"], mesh.shape["emp"]),
        mesh=mesh,
        in_specs=(
            P(),
            P(),
            P("seek", None),
            P("emp", None),
            P(),
            P("seek"),
            P("emp"),
            P("seek"),
            P("emp"),
        ),
        out_specs=(P(("seek", "emp"), None), P(("emp", "seek"), None), P()),
        check_vma=False,
    )
```

```python
import functools

import jax
import jax.numpy as jnp
from jax import lax
from jax.experimental import pallas as pl
from jax.experimental.pallas import tpu as pltpu
from jax.sharding import PartitionSpec as P

E = 256
BLK = 512
LANES = 128
ROWS = 64
GROUPS = BLK // LANES
LOW = -1.0e30
TO_LOG2 = 1.4426950408889634 * E ** (-0.5)
VMEM_LIMIT = 56 * 1024 * 1024


def nt_dot(a, b):
    return lax.dot_general(a, b, (((1,), (1,)), ((), ())), preferred_element_type=jnp.float32)


def tn_dot(a, b):
    return lax.dot_general(a, b, (((0,), (0,)), ((), ())), preferred_element_type=jnp.float32)


def block_ds(index, size):
    return pl.ds(pl.multiple_of(index * size, size), size)


def list_pairs(seek_region, emp_region, seek_at, emp_at, nblocks, eblocks, list_i, list_j):
    list_i[0] = nblocks
    list_j[0] = eblocks

    def visit(p, count):
        i = p // eblocks
        j = lax.rem(p, eblocks)
        list_i[count + 1] = i
        list_j[count + 1] = j
        same = seek_region[seek_at + i] == emp_region[emp_at + j]
        return count + same.astype(jnp.int32)

    count = lax.fori_loop(0, nblocks * eblocks, visit, jnp.int32(0))
    for k in range(1, 4):
        list_i[count + k] = nblocks
        list_j[count + k] = eblocks
    list_i[nblocks * eblocks + 4] = count


def stats_kernel(
    nblocks, eblocks, seek_region, emp_region, seeker, employer, bilinear,
    proj, row_stats, col_stats, list_i, list_j,
    score_a, score_b, row_max, row_sum, col_max, col_sum,
):
    list_pairs(
        seek_region, emp_region, lax.axis_index("seek") * nblocks,
        lax.axis_index("emp") * eblocks, nblocks, eblocks, list_i, list_j,
    )
    count = list_i[nblocks * eblocks + 4]
    col_max[...] = jnp.full_like(col_max, LOW)
    col_sum[...] = jnp.zeros_like(col_sum)

    def project(i, carry):
        rows_at = block_ds(i, BLK)
        proj[rows_at, :] = jnp.dot(
            seeker[rows_at, :], bilinear[...], preferred_element_type=jnp.float32
        ).astype(jnp.bfloat16)
        row_max[rows_at, :] = jnp.full((BLK, LANES), LOW, jnp.float32)
        row_sum[rows_at, :] = jnp.zeros((BLK, LANES), jnp.float32)
        return carry

    lax.fori_loop(0, nblocks, project, 0)
    half = BLK // 2

    def score_half(n, h, out):
        i = jnp.minimum(list_i[n + 1], nblocks - 1)
        j = jnp.minimum(list_j[n + 1], eblocks - 1)
        left = proj[pl.ds(pl.multiple_of(i * BLK + h * half, half), half), :]
        out[h * half : (h + 1) * half, :] = nt_dot(left, employer[block_ds(j, BLK), :])

    def step(n, score, later):
        i = list_i[n + 1]
        j = list_j[n + 1]
        cm = col_max[j]
        cs = col_sum[j]
        for c in range(BLK // ROWS):
            if c in (0, 4):
                score_half(n + 1, c // 4, later)
            part = slice(c * ROWS, (c + 1) * ROWS)
            rows_at = pl.ds(pl.multiple_of(i * BLK + c * ROWS, ROWS), ROWS)
            s = score[part, :] * TO_LOG2
            tall = s.reshape(ROWS // 8, 8, BLK)
            cm_new = jnp.maximum(cm, jnp.max(tall, axis=0))
            cs = cs * jnp.exp2(cm - cm_new) + jnp.sum(jnp.exp2(tall - cm_new[None]), axis=0)
            cm = cm_new
            old = row_max[rows_at, :]
            pieces = [s[:, g * LANES : (g + 1) * LANES] for g in range(GROUPS)]
            new = functools.reduce(jnp.maximum, pieces, old)
            total = row_sum[rows_at, :] * jnp.exp2(old - new)
            for piece in pieces:
                total = total + jnp.exp2(piece - new)
            row_max[rows_at, :] = new
            row_sum[rows_at, :] = total
        col_max[j] = cm
        col_sum[j] = cs

    score_half(0, 0, score_a)
    score_half(0, 1, score_a)

    def two(m, carry):
        step(2 * m, score_a, score_b)
        step(2 * m + 1, score_b, score_a)
        return carry

    lax.fori_loop(0, (count + 1) // 2, two, 0)

    lane = lax.broadcasted_iota(jnp.int32, (BLK, LANES), 1)

    def finish(i, carry):
        rows_at = block_ds(i, BLK)
        lane_max = row_max[rows_at, :]
        top = jnp.max(lane_max, axis=1, keepdims=True)
        total = jnp.sum(row_sum[rows_at, :] * jnp.exp2(lane_max - top), axis=1, keepdims=True)
        both = jnp.where(lane == 0, top, total).T
        row_stats[0, pl.ds(i, 1), :] = both[0:1]
        row_stats[1, pl.ds(i, 1), :] = both[1:2]
        return carry

    lax.fori_loop(0, nblocks, finish, 0)
    for j in range(eblocks):
        cm = col_max[j]
        top = jnp.max(cm, axis=0, keepdims=True)
        total = jnp.sum(col_sum[j] * jnp.exp2(cm - top), axis=0, keepdims=True)
        col_stats[0, j : j + 1, :] = top
        col_stats[1, j : j + 1, :] = total


def entry_barrier(n_seek, n_emp, me_s, me_e):
    barrier = pltpu.get_barrier_semaphore()
    for k in range(1, n_emp):
        pl.semaphore_signal(
            barrier, inc=1, device_id={"emp": lax.rem(me_e + k, n_emp)},
            device_id_type=pl.DeviceIdType.MESH,
        )
    for k in range(1, n_seek):
        pl.semaphore_signal(
            barrier, inc=1, device_id={"seek": lax.rem(me_s + k, n_seek)},
            device_id_type=pl.DeviceIdType.MESH,
        )
    pl.semaphore_wait(barrier, n_emp + n_seek - 2)


def send(src, dst, send_sem, recv_sem, axis, peer):
    return pltpu.make_async_remote_copy(
        src_ref=src, dst_ref=dst, send_sem=send_sem, recv_sem=recv_sem,
        device_id={axis: peer}, device_id_type=pl.DeviceIdType.MESH,
    )


def exchange_kernel(
    n_seek, n_emp, row_stats, col_stats, row_weight, col_weight, row_log, col_log,
    row_pack, col_pack,
    row_buf, col_buf, row_send, row_recv, col_send, col_recv,
):
    me_s = lax.axis_index("seek")
    me_e = lax.axis_index("emp")
    entry_barrier(n_seek, n_emp, me_s, me_e)
    copies = []
    for k in range(1, n_emp):
        copies.append(send(
            row_stats, row_buf.at[k], row_send.at[k], row_recv.at[k],
            "emp", lax.rem(me_e + k, n_emp),
        ))
    for k in range(1, n_seek):
        copies.append(send(
            col_stats, col_buf.at[k], col_send.at[k], col_recv.at[k],
            "seek", lax.rem(me_s + k, n_seek),
        ))
    for copy in copies:
        copy.start()
    for weight, log, pack in ((row_weight, row_log, row_pack), (col_weight, col_log, col_pack)):
        for i in range(pack.shape[0]):
            lanes = slice(i * BLK, (i + 1) * BLK)
            pack[i, 2:3, :] = weight[:, lanes] * E ** (-0.5)
            pack[i, 3:4, :] = log[:, lanes].astype(jnp.float32)
            pack[i, 4:8, :] = jnp.zeros((4, BLK), jnp.float32)
    for copy in copies:
        copy.wait()
    for own, buf, n, pack in (
        (row_stats, row_buf, n_emp, row_pack), (col_stats, col_buf, n_seek, col_pack)
    ):
        top = own[0]
        for k in range(1, n):
            top = jnp.maximum(top, buf[k, 0])
        total = own[1] * jnp.exp2(own[0] - top)
        for k in range(1, n):
            total = total + buf[k, 1] * jnp.exp2(buf[k, 0] - top)
        for i in range(pack.shape[0]):
            pack[i, 0:1, :] = top[i : i + 1]
            pack[i, 1:2, :] = pack[i, 2:3, :] / total[i : i + 1]


def grad_kernel(
    nblocks, eblocks, list_i, list_j, proj, employer, row_pack, col_pack,
    pulled, back,
    score_a, score_b, dscore_a, dscore_b, rt, rc, rw, rl,
):
    count = list_i[nblocks * eblocks + 4]
    row_base = (lax.axis_index("seek") * nblocks * BLK).astype(jnp.float32)
    col_base = (lax.axis_index("emp") * eblocks * BLK).astype(jnp.float32)
    dscore_b[...] = jnp.zeros_like(dscore_b)
    row_ids = lax.broadcasted_iota(jnp.int32, (ROWS, LANES), 0).astype(jnp.float32)
    lane_ids = lax.broadcasted_iota(jnp.int32, (8, LANES), 1).astype(jnp.float32)[0:1]

    def widen(i, carry):
        rows_at = block_ds(i, BLK)
        tall = row_pack[i].T
        for k, wide in enumerate((rt, rc, rw, rl)):
            wide[rows_at, :] = jnp.broadcast_to(tall[:, k : k + 1], (BLK, LANES))
        pulled[rows_at, :] = jnp.zeros((BLK, E), jnp.float32)
        return carry

    lax.fori_loop(0, nblocks, widen, 0)
    pulled[nblocks * BLK :, :] = jnp.zeros((BLK, E), jnp.float32)
    back[...] = jnp.zeros_like(back)
    half = BLK // 2

    def read_at(n):
        return (
            jnp.minimum(list_i[n + 1], nblocks - 1), jnp.minimum(list_j[n + 1], eblocks - 1)
        )

    def score_half(n, h, out):
        i, j = read_at(n)
        left = proj[pl.ds(pl.multiple_of(i * BLK + h * half, half), half), :]
        out[h * half : (h + 1) * half, :] = nt_dot(left, employer[block_ds(j, BLK), :])

    def pull_half(i, jr, h, d):
        at = pl.ds(pl.multiple_of(i * BLK + h * half, half), half)
        pulled[at, :] += jnp.dot(
            d[h * half : (h + 1) * half, :], employer[block_ds(jr, BLK), :],
            preferred_element_type=jnp.float32,
        )

    def back_half(ir, j, h, d):
        at = pl.ds(pl.multiple_of(j * BLK + h * half, half), half)
        back[at, :] += tn_dot(d[:, h * half : (h + 1) * half], proj[block_ds(ir, BLK), :])

    def step(n, score, later, d, done):
        i, j = read_at(n)
        old_i, old_j = list_i[n], list_j[n]
        old_ir, old_jr = read_at(n - 1)
        work = {
            0: lambda: score_half(n + 1, 0, later),
            1: lambda: pull_half(old_i, old_jr, 0, done),
            2: lambda: pull_half(old_i, old_jr, 1, done),
            4: lambda: score_half(n + 1, 1, later),
            5: lambda: back_half(old_ir, old_j, 0, done),
            6: lambda: back_half(old_ir, old_j, 1, done),
        }
        cols = col_pack[j]
        ct, cc, cw = cols[0:1], cols[1:2], cols[2:3]
        cl = cols[3:4] - (row_base + (i * BLK).astype(jnp.float32))
        here = lane_ids + (col_base + (j * BLK).astype(jnp.float32))
        for c in range(BLK // ROWS):
            if c in work:
                work[c]()
            part = slice(c * ROWS, (c + 1) * ROWS)
            rows_at = pl.ds(pl.multiple_of(i * BLK + c * ROWS, ROWS), ROWS)
            rtc, rcc, rwc, rlc = (ref[rows_at, :] for ref in (rt, rc, rw, rl))
            clc = cl - float(c * ROWS)
            for g in range(GROUPS):
                lanes = slice(g * LANES, (g + 1) * LANES)
                t = score[part, lanes] * TO_LOG2
                grad = jnp.exp2(t - rtc) * rcc + jnp.exp2(t - ct[:, lanes]) * cc[:, lanes]
                grad = jnp.where(rlc == here + float(g * LANES), grad - rwc, grad)
                grad = jnp.where(clc[:, lanes] == row_ids, grad - cw[:, lanes], grad)
                d[part, lanes] = grad.astype(jnp.bfloat16)

    score_half(0, 0, score_a)
    score_half(0, 1, score_a)

    def two(m, carry):
        step(2 * m, score_a, score_b, dscore_a, dscore_b)
        step(2 * m + 1, score_b, score_a, dscore_b, dscore_a)
        return carry

    lax.fori_loop(0, (count + 2) // 2, two, 0)


def reduce_kernel(
    n_seek, n_emp, pulled, back, seeker, bilinear,
    seeker_grad, employer_grad, bilinear_grad,
    pair_buf, emp_buf, right_buf, left_buf, bil, bil_emp, bil_seek, bil_all,
    pair_send, pair_recv, emp_send, emp_recv, right_send, right_recv, left_send, left_recv,
    b1_send, b1_recv, b2_send, b2_recv, b3_send, b3_recv, own_rows, own_sem,
):
    me_s = lax.axis_index("seek")
    me_e = lax.axis_index("emp")
    share = seeker_grad.shape[0]
    eshare = employer_grad.shape[0]
    half = n_emp // 2
    mine = me_e // 2
    parity = lax.rem(me_e, 2)
    partner = me_e + 1 - 2 * parity
    mirror = n_seek - 1 - me_s
    entry_barrier(n_seek, n_emp, me_s, me_e)

    def right_copy(k, src):
        return send(
            src, right_buf.at[k], right_send.at[k], right_recv.at[k],
            "seek", lax.rem(me_s + 1, n_seek),
        )

    def left_copy(k, src):
        return send(
            src, left_buf.at[k], left_send.at[k], left_recv.at[k],
            "seek", lax.rem(me_s + n_seek - 1, n_seek),
        )

    def line_step(k):
        for pos, make, buf, target in (
            (me_s, right_copy, right_buf, n_seek - 1 - k + me_s),
            (mirror, left_copy, left_buf, k - mirror),
        ):
            @pl.when(pos == 0)
            def _(make=make, target=target):
                make(k, back.at[block_ds(target, eshare), :]).start()

            if k > 0:
                @pl.when(jnp.logical_and(pos > 0, pos <= k))
                def _(make=make, buf=buf, target=target):
                    make(k - 1, buf.at[k - 1]).wait_recv()
                    buf[k - 1] += back[block_ds(target, eshare), :]
                    make(k, buf.at[k - 1]).start()

    line_step(0)
    fetch = pltpu.make_async_copy(seeker.at[block_ds(me_e, share), :], own_rows, own_sem)
    fetch.start()
    pairs = []
    order = list(range(half - 1, -1, -1))
    for k in range(half):
        target = 2 * lax.rem(mine + k, half) + 1 - parity
        pairs.append(send(
            pulled.at[block_ds(target, share), :], pair_buf.at[k],
            pair_send.at[k], pair_recv.at[k], "emp", partner,
        ))
    for k in order:
        pairs[k].start()
    seconds = {}
    for k in order:
        pairs[k].wait_recv()
        target = 2 * lax.rem(mine + k, half) + parity
        pair_buf[k] += pulled[block_ds(target, share), :]
        if k > 0:
            seconds[k] = send(
                pair_buf.at[k], emp_buf.at[k], emp_send.at[k], emp_recv.at[k], "emp", target
            )
            seconds[k].start()
    for k in range(1, n_seek - 1):
        line_step(k)
    for k in seconds:
        seconds[k].wait_recv()
        pair_buf[0] += emp_buf[k]

    share_rows = pair_buf[0].astype(jnp.bfloat16)
    fetch.wait()
    bil[...] = tn_dot(own_rows[...], share_rows)
    slab = E // n_emp
    b1 = []
    for k in range(1, n_emp):
        peer = lax.rem(me_e + k, n_emp)
        b1.append(send(
            bil.at[block_ds(peer, slab), :], bil_emp.at[k], b1_send.at[k], b1_recv.at[k],
            "emp", peer,
        ))
    for copy in b1:
        copy.start()
    seeker_grad[...] = nt_dot(share_rows, bilinear[...])
    own_slab = block_ds(me_e, slab)
    for copy in b1:
        copy.wait_recv()
    part = bil[own_slab, :]
    for k in range(1, n_emp):
        part = part + bil_emp[k]
    bil_seek[me_s] = part
    b2 = []
    for k in range(1, n_seek):
        b2.append(send(
            bil_seek.at[me_s], bil_seek.at[me_s], b2_send.at[k], b2_recv.at[k],
            "seek", lax.rem(me_s + k, n_seek),
        ))
    for copy in b2:
        copy.start()
    for k in range(1, n_seek):
        slot = bil_seek.at[lax.rem(me_s + n_seek - k, n_seek)]
        send(
            slot, slot, b2_send.at[k], b2_recv.at[k], "seek", lax.rem(me_s + k, n_seek)
        ).wait_recv()
    part = bil_seek[0]
    for k in range(1, n_seek):
        part = part + bil_seek[k]
    bil_all[own_slab, :] = part
    b3 = []
    for k in range(1, n_emp):
        b3.append(send(
            bil_all.at[own_slab, :], bil_all.at[own_slab, :], b3_send.at[k], b3_recv.at[k],
            "emp", lax.rem(me_e + k, n_emp),
        ))
    for copy in b3:
        copy.start()
    for k in range(1, n_emp):
        slot = bil_all.at[block_ds(lax.rem(me_e + n_emp - k, n_emp), slab), :]
        send(
            slot, slot, b3_send.at[k], b3_recv.at[k], "emp", lax.rem(me_e + k, n_emp)
        ).wait_recv()
    bilinear_grad[...] = bil_all[...]

    employer_grad[...] = back[block_ds(me_s, eshare), :]
    last = n_seek - 2
    for pos, make, buf in ((me_s, right_copy, right_buf), (mirror, left_copy, left_buf)):
        @pl.when(pos > 0)
        def _(make=make, buf=buf):
            make(last, buf.at[last]).wait_recv()
            employer_grad[...] += buf[last]

    for copy in pairs + list(seconds.values()) + b1 + b2 + b3:
        copy.wait_send()
    for k in range(n_seek - 1):
        for pos, make, buf in ((me_s, right_copy, right_buf), (mirror, left_copy, left_buf)):
            @pl.when(pos <= k)
            def _(k=k, make=make, buf=buf):
                make(k, buf.at[k]).wait_send()


def vmem():
    return pl.BlockSpec(memory_space=pltpu.VMEM)


def smem():
    return pl.BlockSpec(memory_space=pltpu.SMEM)


def f32(*shape):
    return jax.ShapeDtypeStruct(shape, jnp.float32)


def body(
    n_seek, n_emp, seek_region, emp_region, seeker_emb, employer_emb, bilinear,
    logged_emp, logged_seeker, seek_weight, emp_weight,
):
    seekers = seeker_emb.shape[0]
    employers = employer_emb.shape[0]
    nblocks = seekers // BLK
    eblocks = employers // BLK
    pairs = jax.ShapeDtypeStruct((nblocks * eblocks + 5,), jnp.int32)

    proj, row_stats, col_stats, list_i, list_j = pl.pallas_call(
        functools.partial(stats_kernel, nblocks, eblocks),
        out_shape=(
            jax.ShapeDtypeStruct((seekers, E), jnp.bfloat16),
            f32(2, nblocks, BLK),
            f32(2, eblocks, BLK),
            pairs,
            pairs,
        ),
        in_specs=[smem()] * 2 + [vmem()] * 3,
        out_specs=(vmem(),) * 3 + (smem(),) * 2,
        scratch_shapes=[
            pltpu.VMEM((BLK, BLK), jnp.float32),
            pltpu.VMEM((BLK, BLK), jnp.float32),
            pltpu.VMEM((seekers + BLK, LANES), jnp.float32),
            pltpu.VMEM((seekers + BLK, LANES), jnp.float32),
            pltpu.VMEM((eblocks + 1, 8, BLK), jnp.float32),
            pltpu.VMEM((eblocks + 1, 8, BLK), jnp.float32),
        ],
        compiler_params=pltpu.CompilerParams(vmem_limit_bytes=VMEM_LIMIT),
        name="stats",
    )(seek_region, emp_region, seeker_emb, employer_emb, bilinear)

    row_pack, col_pack = pl.pallas_call(
        functools.partial(exchange_kernel, n_seek, n_emp),
        out_shape=(f32(nblocks, 8, BLK), f32(eblocks, 8, BLK)),
        in_specs=[vmem()] * 6,
        out_specs=(vmem(),) * 2,
        scratch_shapes=[
            pltpu.VMEM((n_emp, 2, nblocks, BLK), jnp.float32),
            pltpu.VMEM((n_seek, 2, eblocks, BLK), jnp.float32),
            pltpu.SemaphoreType.DMA((n_emp,)),
            pltpu.SemaphoreType.DMA((n_emp,)),
            pltpu.SemaphoreType.DMA((n_seek,)),
            pltpu.SemaphoreType.DMA((n_seek,)),
        ],
        compiler_params=pltpu.CompilerParams(collective_id=0, has_side_effects=True),
        name="exchange",
    )(
        row_stats, col_stats, seek_weight.reshape(1, seekers), emp_weight.reshape(1, employers),
        logged_emp.reshape(1, seekers), logged_seeker.reshape(1, employers),
    )

    pulled, back = pl.pallas_call(
        functools.partial(grad_kernel, nblocks, eblocks),
        out_shape=(f32(seekers + BLK, E), f32(employers + BLK, E)),
        in_specs=[smem()] * 2 + [vmem()] * 4,
        out_specs=(vmem(),) * 2,
        scratch_shapes=[pltpu.VMEM((BLK, BLK), jnp.float32)] * 2
        + [pltpu.VMEM((BLK, BLK), jnp.bfloat16)] * 2
        + [pltpu.VMEM((seekers, LANES), jnp.float32)] * 4,
        compiler_params=pltpu.CompilerParams(vmem_limit_bytes=VMEM_LIMIT),
        name="grads",
    )(list_i, list_j, proj, employer_emb, row_pack, col_pack)

    share = seekers // n_emp
    eshare = employers // n_seek
    slab = E // n_emp
    dma = pltpu.SemaphoreType.DMA
    return pl.pallas_call(
        functools.partial(reduce_kernel, n_seek, n_emp),
        out_shape=(f32(share, E), f32(eshare, E), f32(E, E)),
        in_specs=[vmem()] * 2 + [pl.BlockSpec(memory_space=pl.ANY), vmem()],
        out_specs=(vmem(),) * 3,
        scratch_shapes=[
            pltpu.VMEM((n_emp // 2, share, E), jnp.float32),
            pltpu.VMEM((n_emp // 2, share, E), jnp.float32),
            pltpu.VMEM((n_seek - 1, eshare, E), jnp.float32),
            pltpu.VMEM((n_seek - 1, eshare, E), jnp.float32),
            pltpu.VMEM((E, E), jnp.float32),
            pltpu.VMEM((n_emp, slab, E), jnp.float32),
            pltpu.VMEM((n_seek, slab, E), jnp.float32),
            pltpu.VMEM((E, E), jnp.float32),
            dma((n_emp // 2,)), dma((n_emp // 2,)),
            dma((n_emp // 2,)), dma((n_emp // 2,)),
            dma((n_seek - 1,)), dma((n_seek - 1,)),
            dma((n_seek - 1,)), dma((n_seek - 1,)),
            dma((n_emp,)), dma((n_emp,)),
            dma((n_seek,)), dma((n_seek,)),
            dma((n_emp,)), dma((n_emp,)),
            pltpu.VMEM((share, E), jnp.bfloat16), dma,
        ],
        compiler_params=pltpu.CompilerParams(
            collective_id=1, has_side_effects=True, vmem_limit_bytes=VMEM_LIMIT
        ),
        name="reduce",
    )(pulled, back, seeker_emb, bilinear)


def solution(mesh):
    return jax.shard_map(
        functools.partial(body, mesh.shape["seek"], mesh.shape["emp"]),
        mesh=mesh,
        in_specs=(
            P(),
            P(),
            P("seek", None),
            P("emp", None),
            P(),
            P("seek"),
            P("emp"),
            P("seek"),
            P("emp"),
        ),
        out_specs=(P(("seek", "emp"), None), P(("emp", "seek"), None), P()),
        check_vma=False,
    )
```

```python
import functools

import jax
import jax.numpy as jnp
from jax import lax
from jax.experimental import pallas as pl
from jax.experimental.pallas import tpu as pltpu
from jax.sharding import PartitionSpec as P

E = 256
BLK = 512
LANES = 128
ROWS = 64
GROUPS = BLK // LANES
LOW = -1.0e30
TO_LOG2 = 1.4426950408889634 * E ** (-0.5)
VMEM_LIMIT = 56 * 1024 * 1024


def nt_dot(a, b):
    return lax.dot_general(a, b, (((1,), (1,)), ((), ())), preferred_element_type=jnp.float32)


def tn_dot(a, b):
    return lax.dot_general(a, b, (((0,), (0,)), ((), ())), preferred_element_type=jnp.float32)


def block_ds(index, size):
    return pl.ds(pl.multiple_of(index * size, size), size)


def list_pairs(seek_region, emp_region, seek_at, emp_at, nblocks, eblocks, list_i, list_j):
    list_i[0] = nblocks
    list_j[0] = eblocks

    wanted = [emp_region[emp_at + j] for j in range(eblocks)]

    def visit(i, count):
        region = seek_region[seek_at + i]
        for j in range(eblocks):
            list_i[count + 1] = i
            list_j[count + 1] = j
            count = count + (region == wanted[j]).astype(jnp.int32)
        return count

    count = lax.fori_loop(0, nblocks, visit, jnp.int32(0))
    for k in range(1, 4):
        list_i[count + k] = nblocks
        list_j[count + k] = eblocks
    list_i[nblocks * eblocks + 4] = count


def stats_kernel(
    nblocks, eblocks, seek_region, emp_region, seeker, employer, bilinear,
    proj, row_stats, col_stats, list_i, list_j,
    score_a, score_b, row_max, row_sum, col_max, col_sum,
):
    list_pairs(
        seek_region, emp_region, lax.axis_index("seek") * nblocks,
        lax.axis_index("emp") * eblocks, nblocks, eblocks, list_i, list_j,
    )
    count = list_i[nblocks * eblocks + 4]
    col_max[...] = jnp.full_like(col_max, LOW)
    col_sum[...] = jnp.zeros_like(col_sum)

    def project(i, carry):
        rows_at = block_ds(i, BLK)
        proj[rows_at, :] = jnp.dot(
            seeker[rows_at, :], bilinear[...], preferred_element_type=jnp.float32
        ).astype(jnp.bfloat16)
        row_max[rows_at, :] = jnp.full((BLK, LANES), LOW, jnp.float32)
        row_sum[rows_at, :] = jnp.zeros((BLK, LANES), jnp.float32)
        return carry

    lax.fori_loop(0, nblocks, project, 0)
    half = BLK // 2

    def score_half(n, h, out):
        i = jnp.minimum(list_i[n + 1], nblocks - 1)
        j = jnp.minimum(list_j[n + 1], eblocks - 1)
        left = proj[pl.ds(pl.multiple_of(i * BLK + h * half, half), half), :]
        out[h * half : (h + 1) * half, :] = nt_dot(left, employer[block_ds(j, BLK), :])

    def step(n, score, later):
        i = list_i[n + 1]
        j = list_j[n + 1]
        cm = col_max[j]
        cs = col_sum[j]
        for c in range(BLK // ROWS):
            if c in (0, 4):
                score_half(n + 1, c // 4, later)
            part = slice(c * ROWS, (c + 1) * ROWS)
            rows_at = pl.ds(pl.multiple_of(i * BLK + c * ROWS, ROWS), ROWS)
            s = score[part, :] * TO_LOG2
            tall = s.reshape(ROWS // 8, 8, BLK)
            cm_new = jnp.maximum(cm, jnp.max(tall, axis=0))
            cs = cs * jnp.exp2(cm - cm_new) + jnp.sum(jnp.exp2(tall - cm_new[None]), axis=0)
            cm = cm_new
            old = row_max[rows_at, :]
            pieces = [s[:, g * LANES : (g + 1) * LANES] for g in range(GROUPS)]
            new = functools.reduce(jnp.maximum, pieces, old)
            total = row_sum[rows_at, :] * jnp.exp2(old - new)
            for piece in pieces:
                total = total + jnp.exp2(piece - new)
            row_max[rows_at, :] = new
            row_sum[rows_at, :] = total
        col_max[j] = cm
        col_sum[j] = cs

    score_half(0, 0, score_a)
    score_half(0, 1, score_a)

    def two(m, carry):
        step(2 * m, score_a, score_b)
        step(2 * m + 1, score_b, score_a)
        return carry

    lax.fori_loop(0, (count + 1) // 2, two, 0)

    lane = lax.broadcasted_iota(jnp.int32, (BLK, LANES), 1)

    def finish(i, carry):
        rows_at = block_ds(i, BLK)
        lane_max = row_max[rows_at, :]
        top = jnp.max(lane_max, axis=1, keepdims=True)
        total = jnp.sum(row_sum[rows_at, :] * jnp.exp2(lane_max - top), axis=1, keepdims=True)
        both = jnp.where(lane == 0, top, total).T
        row_stats[0, pl.ds(i, 1), :] = both[0:1]
        row_stats[1, pl.ds(i, 1), :] = both[1:2]
        return carry

    lax.fori_loop(0, nblocks, finish, 0)
    for j in range(eblocks):
        cm = col_max[j]
        top = jnp.max(cm, axis=0, keepdims=True)
        total = jnp.sum(col_sum[j] * jnp.exp2(cm - top), axis=0, keepdims=True)
        col_stats[0, j : j + 1, :] = top
        col_stats[1, j : j + 1, :] = total


def entry_barrier(n_seek, n_emp, me_s, me_e):
    barrier = pltpu.get_barrier_semaphore()
    for k in range(1, n_emp):
        pl.semaphore_signal(
            barrier, inc=1, device_id={"emp": lax.rem(me_e + k, n_emp)},
            device_id_type=pl.DeviceIdType.MESH,
        )
    for k in range(1, n_seek):
        pl.semaphore_signal(
            barrier, inc=1, device_id={"seek": lax.rem(me_s + k, n_seek)},
            device_id_type=pl.DeviceIdType.MESH,
        )
    pl.semaphore_wait(barrier, n_emp + n_seek - 2)


def send(src, dst, send_sem, recv_sem, axis, peer):
    return pltpu.make_async_remote_copy(
        src_ref=src, dst_ref=dst, send_sem=send_sem, recv_sem=recv_sem,
        device_id={axis: peer}, device_id_type=pl.DeviceIdType.MESH,
    )


def exchange_kernel(
    n_seek, n_emp, row_stats, col_stats, row_weight, col_weight, row_log, col_log,
    row_pack, col_pack,
    row_buf, col_buf, row_send, row_recv, col_send, col_recv,
):
    me_s = lax.axis_index("seek")
    me_e = lax.axis_index("emp")
    entry_barrier(n_seek, n_emp, me_s, me_e)
    copies = []
    for k in range(1, n_emp):
        copies.append(send(
            row_stats, row_buf.at[k], row_send.at[k], row_recv.at[k],
            "emp", lax.rem(me_e + k, n_emp),
        ))
    for k in range(1, n_seek):
        copies.append(send(
            col_stats, col_buf.at[k], col_send.at[k], col_recv.at[k],
            "seek", lax.rem(me_s + k, n_seek),
        ))
    for copy in copies:
        copy.start()
    for weight, log, pack in ((row_weight, row_log, row_pack), (col_weight, col_log, col_pack)):
        for i in range(pack.shape[0]):
            lanes = slice(i * BLK, (i + 1) * BLK)
            pack[i, 2:3, :] = weight[:, lanes] * E ** (-0.5)
            pack[i, 3:4, :] = log[:, lanes].astype(jnp.float32)
            pack[i, 4:8, :] = jnp.zeros((4, BLK), jnp.float32)
    for copy in copies:
        copy.wait()
    for own, buf, n, pack in (
        (row_stats, row_buf, n_emp, row_pack), (col_stats, col_buf, n_seek, col_pack)
    ):
        top = own[0]
        for k in range(1, n):
            top = jnp.maximum(top, buf[k, 0])
        total = own[1] * jnp.exp2(own[0] - top)
        for k in range(1, n):
            total = total + buf[k, 1] * jnp.exp2(buf[k, 0] - top)
        for i in range(pack.shape[0]):
            pack[i, 0:1, :] = top[i : i + 1]
            pack[i, 1:2, :] = pack[i, 2:3, :] / total[i : i + 1]


def grad_kernel(
    nblocks, eblocks, list_i, list_j, proj, employer, row_pack, col_pack,
    pulled, back,
    score_a, score_b, dscore_a, dscore_b, rt, rc, rw, rl,
):
    count = list_i[nblocks * eblocks + 4]
    row_base = (lax.axis_index("seek") * nblocks * BLK).astype(jnp.float32)
    col_base = (lax.axis_index("emp") * eblocks * BLK).astype(jnp.float32)
    dscore_b[...] = jnp.zeros_like(dscore_b)
    row_ids = lax.broadcasted_iota(jnp.int32, (ROWS, LANES), 0).astype(jnp.float32)
    lane_ids = lax.broadcasted_iota(jnp.int32, (8, LANES), 1).astype(jnp.float32)[0:1]

    def widen(i, carry):
        rows_at = block_ds(i, BLK)
        tall = row_pack[i].T
        for k, wide in enumerate((rt, rc, rw, rl)):
            wide[rows_at, :] = jnp.broadcast_to(tall[:, k : k + 1], (BLK, LANES))
        pulled[rows_at, :] = jnp.zeros((BLK, E), jnp.float32)
        return carry

    lax.fori_loop(0, nblocks, widen, 0)
    pulled[nblocks * BLK :, :] = jnp.zeros((BLK, E), jnp.float32)
    back[...] = jnp.zeros_like(back)
    half = BLK // 2

    def read_at(n):
        return (
            jnp.minimum(list_i[n + 1], nblocks - 1), jnp.minimum(list_j[n + 1], eblocks - 1)
        )

    def score_half(n, h, out):
        i, j = read_at(n)
        left = proj[pl.ds(pl.multiple_of(i * BLK + h * half, half), half), :]
        out[h * half : (h + 1) * half, :] = nt_dot(left, employer[block_ds(j, BLK), :])

    def pull_half(i, jr, h, d):
        at = pl.ds(pl.multiple_of(i * BLK + h * half, half), half)
        pulled[at, :] += jnp.dot(
            d[h * half : (h + 1) * half, :], employer[block_ds(jr, BLK), :],
            preferred_element_type=jnp.float32,
        )

    def back_half(ir, j, h, d):
        at = pl.ds(pl.multiple_of(j * BLK + h * half, half), half)
        back[at, :] += tn_dot(d[:, h * half : (h + 1) * half], proj[block_ds(ir, BLK), :])

    def step(n, score, later, d, done):
        i, j = read_at(n)
        old_i, old_j = list_i[n], list_j[n]
        old_ir, old_jr = read_at(n - 1)
        work = {
            0: lambda: score_half(n + 1, 0, later),
            1: lambda: pull_half(old_i, old_jr, 0, done),
            2: lambda: pull_half(old_i, old_jr, 1, done),
            4: lambda: score_half(n + 1, 1, later),
            5: lambda: back_half(old_ir, old_j, 0, done),
            6: lambda: back_half(old_ir, old_j, 1, done),
        }
        cols = col_pack[j]
        ct, cc, cw = cols[0:1], cols[1:2], cols[2:3]
        cl = cols[3:4] - (row_base + (i * BLK).astype(jnp.float32))
        here = lane_ids + (col_base + (j * BLK).astype(jnp.float32))
        for c in range(BLK // ROWS):
            if c in work:
                work[c]()
            part = slice(c * ROWS, (c + 1) * ROWS)
            rows_at = pl.ds(pl.multiple_of(i * BLK + c * ROWS, ROWS), ROWS)
            rtc, rcc, rwc, rlc = (ref[rows_at, :] for ref in (rt, rc, rw, rl))
            clc = cl - float(c * ROWS)
            for g in range(GROUPS):
                lanes = slice(g * LANES, (g + 1) * LANES)
                t = score[part, lanes] * TO_LOG2
                grad = jnp.exp2(t - rtc) * rcc + jnp.exp2(t - ct[:, lanes]) * cc[:, lanes]
                grad = jnp.where(rlc == here + float(g * LANES), grad - rwc, grad)
                grad = jnp.where(clc[:, lanes] == row_ids, grad - cw[:, lanes], grad)
                d[part, lanes] = grad.astype(jnp.bfloat16)

    score_half(0, 0, score_a)
    score_half(0, 1, score_a)

    def two(m, carry):
        step(2 * m, score_a, score_b, dscore_a, dscore_b)
        step(2 * m + 1, score_b, score_a, dscore_b, dscore_a)
        return carry

    lax.fori_loop(0, (count + 2) // 2, two, 0)


def reduce_kernel(
    n_seek, n_emp, pulled, back, seeker,
    share_out, employer_grad, bilinear_grad,
    pair_buf, emp_buf, right_buf, left_buf, bil, bil_emp, bil_seek, bil_all,
    pair_send, pair_recv, emp_send, emp_recv, right_send, right_recv, left_send, left_recv,
    b1_send, b1_recv, b2_send, b2_recv, b3_send, b3_recv, own_rows, own_sem,
    own_pull, own_pull_sem, own_back, own_back_sem,
):
    me_s = lax.axis_index("seek")
    me_e = lax.axis_index("emp")
    share = share_out.shape[0]
    eshare = employer_grad.shape[0]
    half = n_emp // 2
    mine = me_e // 2
    parity = lax.rem(me_e, 2)
    partner = me_e + 1 - 2 * parity
    mirror = n_seek - 1 - me_s
    fetch_rows = pltpu.make_async_copy(seeker.at[block_ds(me_e, share), :], own_rows, own_sem)
    fetch_back = pltpu.make_async_copy(
        back.at[pl.ds(0, eshare * n_seek), :], own_back, own_back_sem
    )
    fetch_pull = [
        pltpu.make_async_copy(
            pulled.at[block_ds(2 * lax.rem(mine + k, half) + parity, share), :],
            own_pull.at[k], own_pull_sem.at[k],
        )
        for k in range(half)
    ]
    entry_barrier(n_seek, n_emp, me_s, me_e)

    def right_copy(k, src):
        return send(
            src, right_buf.at[k], right_send.at[k], right_recv.at[k],
            "seek", lax.rem(me_s + 1, n_seek),
        )

    def left_copy(k, src):
        return send(
            src, left_buf.at[k], left_send.at[k], left_recv.at[k],
            "seek", lax.rem(me_s + n_seek - 1, n_seek),
        )

    def line_step(k):
        for pos, make, buf, target in (
            (me_s, right_copy, right_buf, n_seek - 1 - k + me_s),
            (mirror, left_copy, left_buf, k - mirror),
        ):
            @pl.when(pos == 0)
            def _(make=make, target=target):
                make(k, back.at[block_ds(target, eshare), :]).start()

            if k > 0:
                @pl.when(jnp.logical_and(pos > 0, pos <= k))
                def _(make=make, buf=buf, target=target):
                    make(k - 1, buf.at[k - 1]).wait_recv()
                    buf[k - 1] += own_back[block_ds(target, eshare), :]
                    make(k, buf.at[k - 1]).start()

    line_step(0)
    pairs = []
    order = list(range(half - 1, -1, -1))
    for k in range(half):
        target = 2 * lax.rem(mine + k, half) + 1 - parity
        pairs.append(send(
            pulled.at[block_ds(target, share), :], pair_buf.at[k],
            pair_send.at[k], pair_recv.at[k], "emp", partner,
        ))
    for k in order:
        pairs[k].start()
    for k in order:
        fetch_pull[k].start()
    fetch_back.start()
    fetch_rows.start()
    seconds = {}
    for k in order:
        pairs[k].wait_recv()
        target = 2 * lax.rem(mine + k, half) + parity
        fetch_pull[k].wait()
        pair_buf[k] += own_pull[k]
        if k > 0:
            seconds[k] = send(
                pair_buf.at[k], emp_buf.at[k], emp_send.at[k], emp_recv.at[k], "emp", target
            )
            seconds[k].start()
    fetch_back.wait()
    for k in range(1, n_seek - 1):
        line_step(k)
    for k in seconds:
        seconds[k].wait_recv()
        pair_buf[0] += emp_buf[k]

    share_rows = pair_buf[0].astype(jnp.bfloat16)
    share_out[...] = share_rows
    fetch_rows.wait()
    bil[...] = tn_dot(own_rows[...], share_rows)
    slab = E // n_emp
    b1 = []
    for k in range(1, n_emp):
        peer = lax.rem(me_e + k, n_emp)
        b1.append(send(
            bil.at[block_ds(peer, slab), :], bil_emp.at[k], b1_send.at[k], b1_recv.at[k],
            "emp", peer,
        ))
    for copy in b1:
        copy.start()
    own_slab = block_ds(me_e, slab)
    for copy in b1:
        copy.wait_recv()
    part = bil[own_slab, :]
    for k in range(1, n_emp):
        part = part + bil_emp[k]
    bil_seek[me_s] = part
    b2 = []
    for k in range(1, n_seek):
        b2.append(send(
            bil_seek.at[me_s], bil_seek.at[me_s], b2_send.at[k], b2_recv.at[k],
            "seek", lax.rem(me_s + k, n_seek),
        ))
    for copy in b2:
        copy.start()
    for k in range(1, n_seek):
        slot = bil_seek.at[lax.rem(me_s + n_seek - k, n_seek)]
        send(
            slot, slot, b2_send.at[k], b2_recv.at[k], "seek", lax.rem(me_s + k, n_seek)
        ).wait_recv()
    part = bil_seek[0]
    for k in range(1, n_seek):
        part = part + bil_seek[k]
    bil_all[own_slab, :] = part
    b3 = []
    for k in range(1, n_emp):
        b3.append(send(
            bil_all.at[own_slab, :], bil_all.at[own_slab, :], b3_send.at[k], b3_recv.at[k],
            "emp", lax.rem(me_e + k, n_emp),
        ))
    for copy in b3:
        copy.start()
    for k in range(1, n_emp):
        slot = bil_all.at[block_ds(lax.rem(me_e + n_emp - k, n_emp), slab), :]
        send(
            slot, slot, b3_send.at[k], b3_recv.at[k], "emp", lax.rem(me_e + k, n_emp)
        ).wait_recv()
    bilinear_grad[...] = bil_all[...]

    employer_grad[...] = own_back[block_ds(me_s, eshare), :]
    last = n_seek - 2
    for pos, make, buf in ((me_s, right_copy, right_buf), (mirror, left_copy, left_buf)):
        @pl.when(pos > 0)
        def _(make=make, buf=buf):
            make(last, buf.at[last]).wait_recv()
            employer_grad[...] += buf[last]

    for copy in pairs + list(seconds.values()) + b1 + b2 + b3:
        copy.wait_send()
    for k in range(n_seek - 1):
        for pos, make, buf in ((me_s, right_copy, right_buf), (mirror, left_copy, left_buf)):
            @pl.when(pos <= k)
            def _(k=k, make=make, buf=buf):
                make(k, buf.at[k]).wait_send()


def finish_kernel(
    share_rows, bilinear, employer_part, bilinear_part, seeker_grad, employer_grad, bilinear_grad
):
    seeker_grad[...] = nt_dot(share_rows[...], bilinear[...])
    employer_grad[...] = employer_part[...]
    bilinear_grad[...] = bilinear_part[...]


def vmem():
    return pl.BlockSpec(memory_space=pltpu.VMEM)


def smem():
    return pl.BlockSpec(memory_space=pltpu.SMEM)


def f32(*shape):
    return jax.ShapeDtypeStruct(shape, jnp.float32)


def body(
    n_seek, n_emp, seek_region, emp_region, seeker_emb, employer_emb, bilinear,
    logged_emp, logged_seeker, seek_weight, emp_weight,
):
    seekers = seeker_emb.shape[0]
    employers = employer_emb.shape[0]
    nblocks = seekers // BLK
    eblocks = employers // BLK
    pairs = jax.ShapeDtypeStruct((nblocks * eblocks + 5,), jnp.int32)

    proj, row_stats, col_stats, list_i, list_j = pl.pallas_call(
        functools.partial(stats_kernel, nblocks, eblocks),
        out_shape=(
            jax.ShapeDtypeStruct((seekers, E), jnp.bfloat16),
            f32(2, nblocks, BLK),
            f32(2, eblocks, BLK),
            pairs,
            pairs,
        ),
        in_specs=[smem()] * 2 + [vmem()] * 3,
        out_specs=(vmem(),) * 3 + (smem(),) * 2,
        scratch_shapes=[
            pltpu.VMEM((BLK, BLK), jnp.float32),
            pltpu.VMEM((BLK, BLK), jnp.float32),
            pltpu.VMEM((seekers + BLK, LANES), jnp.float32),
            pltpu.VMEM((seekers + BLK, LANES), jnp.float32),
            pltpu.VMEM((eblocks + 1, 8, BLK), jnp.float32),
            pltpu.VMEM((eblocks + 1, 8, BLK), jnp.float32),
        ],
        compiler_params=pltpu.CompilerParams(vmem_limit_bytes=VMEM_LIMIT),
        name="stats",
    )(seek_region, emp_region, seeker_emb, employer_emb, bilinear)

    row_pack, col_pack = pl.pallas_call(
        functools.partial(exchange_kernel, n_seek, n_emp),
        out_shape=(f32(nblocks, 8, BLK), f32(eblocks, 8, BLK)),
        in_specs=[vmem()] * 6,
        out_specs=(vmem(),) * 2,
        scratch_shapes=[
            pltpu.VMEM((n_emp, 2, nblocks, BLK), jnp.float32),
            pltpu.VMEM((n_seek, 2, eblocks, BLK), jnp.float32),
            pltpu.SemaphoreType.DMA((n_emp,)),
            pltpu.SemaphoreType.DMA((n_emp,)),
            pltpu.SemaphoreType.DMA((n_seek,)),
            pltpu.SemaphoreType.DMA((n_seek,)),
        ],
        compiler_params=pltpu.CompilerParams(collective_id=0, has_side_effects=True),
        name="exchange",
    )(
        row_stats, col_stats, seek_weight.reshape(1, seekers), emp_weight.reshape(1, employers),
        logged_emp.reshape(1, seekers), logged_seeker.reshape(1, employers),
    )

    pulled, back = pl.pallas_call(
        functools.partial(grad_kernel, nblocks, eblocks),
        out_shape=(f32(seekers + BLK, E), f32(employers + BLK, E)),
        in_specs=[smem()] * 2 + [vmem()] * 4,
        out_specs=(vmem(),) * 2,
        scratch_shapes=[pltpu.VMEM((BLK, BLK), jnp.float32)] * 2
        + [pltpu.VMEM((BLK, BLK), jnp.bfloat16)] * 2
        + [pltpu.VMEM((seekers, LANES), jnp.float32)] * 4,
        compiler_params=pltpu.CompilerParams(vmem_limit_bytes=VMEM_LIMIT),
        name="grads",
    )(list_i, list_j, proj, employer_emb, row_pack, col_pack)

    share = seekers // n_emp
    eshare = employers // n_seek
    slab = E // n_emp
    dma = pltpu.SemaphoreType.DMA
    share_rows, employer_part, bilinear_part = pl.pallas_call(
        functools.partial(reduce_kernel, n_seek, n_emp),
        out_shape=(
            jax.ShapeDtypeStruct((share, E), jnp.bfloat16), f32(eshare, E), f32(E, E)
        ),
        in_specs=[pl.BlockSpec(memory_space=pl.ANY)] * 3,
        out_specs=(vmem(),) * 3,
        scratch_shapes=[
            pltpu.VMEM((n_emp // 2, share, E), jnp.float32),
            pltpu.VMEM((n_emp // 2, share, E), jnp.float32),
            pltpu.VMEM((n_seek - 1, eshare, E), jnp.float32),
            pltpu.VMEM((n_seek - 1, eshare, E), jnp.float32),
            pltpu.VMEM((E, E), jnp.float32),
            pltpu.VMEM((n_emp, slab, E), jnp.float32),
            pltpu.VMEM((n_seek, slab, E), jnp.float32),
            pltpu.VMEM((E, E), jnp.float32),
            dma((n_emp // 2,)), dma((n_emp // 2,)),
            dma((n_emp // 2,)), dma((n_emp // 2,)),
            dma((n_seek - 1,)), dma((n_seek - 1,)),
            dma((n_seek - 1,)), dma((n_seek - 1,)),
            dma((n_emp,)), dma((n_emp,)),
            dma((n_seek,)), dma((n_seek,)),
            dma((n_emp,)), dma((n_emp,)),
            pltpu.VMEM((share, E), jnp.bfloat16), dma,
            pltpu.VMEM((n_emp // 2, share, E), jnp.float32), dma((n_emp // 2,)),
            pltpu.VMEM((employers, E), jnp.float32), dma,
        ],
        compiler_params=pltpu.CompilerParams(
            collective_id=1, has_side_effects=True, vmem_limit_bytes=VMEM_LIMIT
        ),
        name="reduce",
    )(pulled, back, seeker_emb)
    return pl.pallas_call(
        finish_kernel,
        out_shape=(f32(share, E), f32(eshare, E), f32(E, E)),
        in_specs=[vmem()] * 4,
        out_specs=(vmem(),) * 3,
        name="finish",
    )(share_rows, bilinear, employer_part, bilinear_part)


def solution(mesh):
    return jax.shard_map(
        functools.partial(body, mesh.shape["seek"], mesh.shape["emp"]),
        mesh=mesh,
        in_specs=(
            P(),
            P(),
            P("seek", None),
            P("emp", None),
            P(),
            P("seek"),
            P("emp"),
            P("seek"),
            P("emp"),
        ),
        out_specs=(P(("seek", "emp"), None), P(("emp", "seek"), None), P()),
        check_vma=False,
    )
```
